512 devices in a mesh: box: 32 (over x, y), dir: 16 (over z, core).
Axes of the slice: x: 4, y: 8, z: 8, core: 2. Of those that a mesh axis runs over, the one named last changes fastest.
Arguments:
- currents: bfloat16 [8192, 8, 128], P(('box', 'dir')), may hold values from -6 to 6
- positions: bfloat16 [8192, 3, 128], P(('box', 'dir')), may hold values from -2 to 2
- radiation: bfloat16 [128, 256], replicated, may hold values from -0.5 to 0.5
- interp_index: int32 [512, 4], replicated, may hold values from 0 to 127
- interp_weight: float32 [512, 4], replicated, may hold values from -3 to 3
- child_phase: float32 [8, 512], replicated, may hold values from -3.140625 to 3.140625
- near_src: int32 [8192, 27], P(('box', 'dir')), may hold values from 0 to 8191, as said below
- trans_src: int32 [1024, 32], P('box'), may hold values from 0 to 1023, as said below
- trans_id: int32 [1024, 32], P('box'), may hold values from 0 to 315
- trans_count: int32 [1024], P('box'), may hold values from 16 to 32, as said below
- trans_table: float32 [316, 2, 512], replicated, may hold values from -0.009 to 0.009
Outputs:
- field: float32 [8192, 8, 128], P(('box', 'dir'))
The draws below stay inside these ranges and needn't reach their ends.
Inputs may be any that keep to these rules, and one draw needn't show every extreme that they name: `near_src`: entry 0 of row i is i itself; every entry lies in the block of 16 boxes that holds i or in a block beside it. `trans_src`: every entry lies in the block of 32 parents that holds the row's parent or in a block beside it. Entries at and after trans_count are ignored; some parent in every block of 32 has 32.
All inputs are finite; a program needn't handle non-finite values.
Results may differ from the reference program's by a relative error of at most 0.0045.
Values may be sent and summed in bfloat16 or wider, within the bound.
A program may use at most 64 MiB of HBM per device.

```python
import math
import jax
import jax.numpy as jnp
from jax import lax

BOX_DEV = 16
P_SIZE = 128
W = 8
K1 = 128
K = 512
STEN = 4
NN = 27
NT = 32
NTAB = 316
NBOX = 8192
NPAR = 1024
GROUP = 32


def window_sources(key, total, block, entries):
    index = jnp.arange(total, dtype=jnp.int32)
    group_idx = index // block
    lower = jnp.maximum(group_idx - 1, 0) * block
    upper = jnp.minimum(group_idx + 2, total // block) * block
    offsets = jax.random.randint(key, (total, entries), 0, 1 << 30, dtype=jnp.int32)
    return lower[:, None] + offsets % (upper - lower)[:, None]


def draw_positions(key, part):
    return jax.random.uniform(jax.random.fold_in(key, 41), (NBOX, 3, P_SIZE), jnp.float32, -2.0, 2.0).astype(jnp.bfloat16)


def draw_near_src(key, part):
    sources = window_sources(jax.random.fold_in(key, 11), NBOX, BOX_DEV, NN)
    return sources.at[:, 0].set(jnp.arange(NBOX, dtype=jnp.int32))


def draw_trans_src(key, part):
    return window_sources(jax.random.fold_in(key, 23), NPAR, GROUP, NT)


def draw_trans_count(key, part):
    counts = jax.random.randint(jax.random.fold_in(key, 31), (NPAR,), NT // 2, NT + 1, dtype=jnp.int32)
    index = jnp.arange(NPAR, dtype=jnp.int32)
    return jnp.where(index % GROUP == 0, NT, counts)


def set_ends(drawn, key, smallest, high):
    spot = [jax.random.randint(jax.random.fold_in(key, axis), (), 0, length) for axis, length in enumerate(drawn.shape)]
    longest = drawn.shape.index(max(drawn.shape))
    neighbour = spot[:longest] + [(spot[longest] + 1) % drawn.shape[longest]] + spot[longest + 1:]
    return drawn.at[tuple(spot)].set(smallest).at[tuple(neighbour)].set(high)


def block_levels(own_key, shape, cuts, least, largest):
    loudness, own = 1.0, jax.random.fold_in(own_key, 6)
    for axis_at, parts in cuts:
        heights = jnp.exp(jax.random.uniform(jax.random.fold_in(own, axis_at), (parts,), jnp.float32, least / len(cuts), largest / len(cuts)))
        loudness = loudness * jnp.repeat(heights, shape[axis_at] // parts).reshape([-1 if axis == axis_at else 1 for axis in range(len(shape))])
    return loudness


def centred(stream_key, shape, spread, most, split=(), kind=jnp.bfloat16):
    values = spread * jax.random.normal(stream_key, shape, jnp.float32)
    if split:
        values = values * block_levels(stream_key, shape, split, -0.22, 0.18)
    return jnp.clip(values, -most, most).astype(kind)


def setup_inputs(seed: int = 0) -> dict:
    key_list = jax.random.split(jax.random.key(seed), 12)
    currents = centred(key_list[0], (NBOX, W, P_SIZE), 1.0, 6.0, ((0, 512),))
    positions = draw_positions(jax.random.fold_in(key_list[11], 71), 0)
    radiation = centred(key_list[2], (P_SIZE, 2 * K1), P_SIZE ** -0.5, 0.5)
    interp_index = set_ends(jax.random.randint(key_list[3], (K, STEN), 0, K1), jax.random.fold_in(key_list[3], 1), 0, K1 - 1).astype(jnp.int32)
    interp_weight = centred(key_list[4], (K, STEN), 0.5, 3.0, (), jnp.float32)
    child_phase = jnp.clip(jax.random.uniform(key_list[5], (8, K), jnp.float32, -3.140625, 3.140625), -3.140625, 3.140625)
    near_src = draw_near_src(jax.random.fold_in(key_list[11], 71), 0)
    trans_src = draw_trans_src(jax.random.fold_in(key_list[11], 71), 0)
    trans_id = set_ends(jax.random.randint(key_list[8], (NPAR, NT), 0, NTAB), jax.random.fold_in(key_list[8], 1), 0, NTAB - 1).astype(jnp.int32)
    trans_count = draw_trans_count(jax.random.fold_in(key_list[11], 71), 0)
    trans_table = centred(key_list[10], (NTAB, 2, K), 0.0015, 0.009, (), jnp.float32)
    return dict(currents=currents, positions=positions, radiation=radiation, interp_index=interp_index, interp_weight=interp_weight, child_phase=child_phase, near_src=near_src, trans_src=trans_src, trans_id=trans_id, trans_count=trans_count, trans_table=trans_table)


def interp_matrix(interp_index, interp_weight, leaf_dirs):
    columns = jnp.arange(leaf_dirs, dtype=jnp.int32)
    matches = (interp_index[:, :, None] == columns[None, None, :]).astype(jnp.float32)
    return lax.optimization_barrier(jnp.sum(interp_weight[:, :, None] * matches, axis=1)).T

def near_tiles(own_pos, src_pos):
    entries = src_pos.shape[1]
    width = src_pos.shape[3]
    dist_sq = jnp.zeros((own_pos.shape[0], entries, width, width), jnp.float32)
    for axis_num in range(3):
        offset = own_pos[:, None, axis_num, :, None] - src_pos[:, :, axis_num, None, :]
        dist_sq = dist_sq + offset * offset
    distance = jnp.sqrt(dist_sq)
    factor = 1.0 / math.sqrt(entries * width)
    return (jnp.cos(4.0 * distance) / (distance + 0.5) * factor).astype(jnp.bfloat16)

def translate(window, sources, list_ids, counts, trans_tab):
    spectra = window[sources].astype(jnp.float32)
    coeff = trans_tab[list_ids]
    entries = jnp.arange(sources.shape[1], dtype=jnp.int32)
    live_mask = (entries[None, :] < counts[:, None]).astype(jnp.float32)
    coeff_re = coeff[:, :, 0, None, :] * live_mask[:, :, None, None]
    coeff_im = coeff[:, :, 1, None, :] * live_mask[:, :, None, None]
    real_part = lax.optimization_barrier(jnp.sum(coeff_re * spectra[:, :, 0] - coeff_im * spectra[:, :, 1], axis=1))
    imag_part = lax.optimization_barrier(jnp.sum(coeff_re * spectra[:, :, 1] + coeff_im * spectra[:, :, 0], axis=1))
    return jnp.stack([real_part, imag_part], axis=1)

def reference(currents, positions, radiation, interp_index, interp_weight, child_phase, near_src, trans_src, trans_id, trans_count, trans_table):

    def near_block(packed):
        box_ids, src_ids = packed
        own_pos = positions[box_ids].astype(jnp.float32)
        src_pos = positions[src_ids].astype(jnp.float32)
        src_x = currents[src_ids].astype(jnp.float32)
        tiles = near_tiles(own_pos, src_pos).astype(jnp.float32)
        return jnp.einsum('bemn,bewn->bwm', tiles, src_x)
    box_ids = jnp.arange(NBOX, dtype=jnp.int32).reshape(-1, 16)
    near_field = lax.map(near_block, (box_ids, near_src.reshape(-1, 16, NN))).reshape(NBOX, W, P_SIZE)
    imatrix = interp_matrix(interp_index, interp_weight, K1).astype(jnp.bfloat16)
    leaf = jnp.dot(currents.reshape(NBOX * W, P_SIZE), radiation, preferred_element_type=jnp.float32).astype(jnp.bfloat16)
    up_re = jnp.dot(leaf[:, :K1], imatrix, preferred_element_type=jnp.float32).reshape(NPAR, 8, W, K)
    up_im = jnp.dot(leaf[:, K1:], imatrix, preferred_element_type=jnp.float32).reshape(NPAR, 8, W, K)
    cos_phase = jnp.cos(child_phase)[None, :, None, :]
    sin_phase = jnp.sin(child_phase)[None, :, None, :]
    parent_re = lax.optimization_barrier(jnp.sum(cos_phase * up_re - sin_phase * up_im, axis=1))
    parent_im = lax.optimization_barrier(jnp.sum(sin_phase * up_re + cos_phase * up_im, axis=1))
    parent = lax.optimization_barrier(jnp.stack([parent_re, parent_im], axis=1).astype(jnp.bfloat16))

    def trans_block(packed):
        sources, list_ids, counts = packed
        return translate(parent, sources, list_ids, counts, trans_table)
    local_field = lax.map(trans_block, (trans_src.reshape(-1, GROUP, NT), trans_id.reshape(-1, GROUP, NT), trans_count.reshape(-1, GROUP)))
    local_field = lax.optimization_barrier(local_field.reshape(NPAR, 2, W, K).astype(jnp.bfloat16)).astype(jnp.float32)
    loc_re = local_field[:, 0][:, None]
    loc_im = local_field[:, 1][:, None]
    down_re = (cos_phase * loc_re + sin_phase * loc_im).reshape(NBOX * W, K).astype(jnp.bfloat16)
    down_im = (cos_phase * loc_im - sin_phase * loc_re).reshape(NBOX * W, K).astype(jnp.bfloat16)
    in_re = jnp.dot(down_re, imatrix.T, preferred_element_type=jnp.float32)
    in_im = jnp.dot(down_im, imatrix.T, preferred_element_type=jnp.float32)
    incoming = jnp.concatenate([in_re, in_im], axis=1).astype(jnp.bfloat16)
    far_field = lax.dot_general(incoming, radiation, (((1,), (1,)), ((), ())), preferred_element_type=jnp.float32)
    return near_field + far_field.reshape(NBOX, W, P_SIZE)
```

```python
import functools
import math

import jax
import jax.numpy as jnp
from jax import lax
from jax.experimental import pallas as pl
from jax.experimental.pallas import tpu as pltpu
from jax.sharding import PartitionSpec as P

F = jnp.float32
BF = jnp.bfloat16
MESH = pl.DeviceIdType.MESH
NT_DIMS = (((1,), (1,)), ((), ()))

TURN = 4.0 / (2.0 * math.pi)
SIN_TURN = (6.283164044284151, -41.33714236874864, 81.34076881229882, -70.99343258230081)
SIN_TURN_LONG = (
    6.283185160089382,
    -41.34165503139618,
    81.60100407210419,
    -76.54978226888187,
    39.536705889889106,
)
TINY = 2e-6

SPREAD_AT = 2
TRANSLATE_AT = 5
RETURN_AT = 6


def cos_turns(turns):
    z = 0.25 - jnp.abs(turns - jnp.round(turns))
    v = z * z
    acc = jnp.full_like(v, SIN_TURN_LONG[-1])
    for c in SIN_TURN_LONG[-2::-1]:
        acc = acc * v + c
    return acc * z


def near_tile(dist_sq):
    turns = dist_sq * lax.rsqrt(jnp.maximum(dist_sq, TINY))
    z = 0.25 - jnp.abs(turns - jnp.round(turns))
    ratio = (z / (turns + 0.5 * TURN)).astype(BF)
    v = z.astype(BF)
    v = v * v
    coefs = [jnp.asarray(c / math.pi, BF) for c in SIN_TURN]
    acc = v * coefs[-1] + coefs[-2]
    for c in coefs[-3::-1]:
        acc = acc * v + c
    return acc * ratio


def inside(index, size):
    return jnp.minimum(jnp.maximum(index, 0), size - 1)


def three_parts(x):
    high = x.astype(BF).astype(F)
    rest = x - high
    mid = rest.astype(BF).astype(F)
    return high, mid, rest - mid


def kernel(
    dims,
    near_src,
    trans_src,
    trans_id,
    trans_count,
    cur,
    pos,
    rad,
    idx,
    wgt,
    phase,
    table,
    out,
    halo_x,
    halo_p,
    tab,
    imat,
    stage,
    window,
    loc,
    back,
    rows32,
    own32,
    src_tab,
    x_tab,
    own_tab,
    near,
    tab_sem,
    hs_sem,
    hr_sem,
    gs_sem,
    gr_sem,
    ss_sem,
    sr_sem,
    bs_sem,
    br_sem,
):
    n_box, n_dir, boxes, entries, trans_entries, ops = dims
    box = lax.axis_index("box")
    d = lax.axis_index("dir")
    me = box * n_dir + d
    n_dev = n_box * n_dir
    quarter = lax.rem(d, 4)
    fourth = d // 4
    nxt = lax.rem(me + 1, n_dev)
    prv = lax.rem(me + n_dev - 1, n_dev)
    nxt_id = (nxt // n_dir, lax.rem(nxt, n_dir))
    prv_id = (prv // n_dir, lax.rem(prv, n_dir))
    up_id = (lax.rem(box + 1, n_box), d)
    down_id = (lax.rem(box + n_box - 1, n_box), d)

    def peer(k):
        return lax.rem(d + k, n_dir)

    barrier = pltpu.get_barrier_semaphore()
    for to in (nxt_id, prv_id, up_id, down_id):
        pl.semaphore_signal(barrier, inc=1, device_id=to, device_id_type=MESH)
    for k in range(1, n_dir):
        pl.semaphore_signal(barrier, inc=1, device_id=(box, peer(k)), device_id_type=MESH)

    lanes = pl.ds(pl.multiple_of(quarter * 128, 128), 128)
    tab_copy = pltpu.make_async_copy(table.at[:, :, lanes], tab.at[pl.ds(0, ops)], tab_sem)
    tab_copy.start()

    row = lax.broadcasted_iota(jnp.int32, (128, 512), 0)
    acc = jnp.zeros((128, 512), F)
    for s in range(4):
        acc = acc + jnp.where(idx[s : s + 1, :] == row, wgt[s : s + 1, :], 0.0)
    imat[...] = acc.astype(BF)
    leaf = jnp.dot(cur[...], rad[...], preferred_element_type=F).astype(BF)

    pl.semaphore_wait(barrier, n_dir + 3)

    def halo(side, to):
        return (
            pltpu.make_async_remote_copy(
                src_ref=cur,
                dst_ref=halo_x.at[side],
                send_sem=hs_sem.at[side],
                recv_sem=hr_sem.at[side],
                device_id=to,
                device_id_type=MESH,
            ),
            pltpu.make_async_remote_copy(
                src_ref=pos,
                dst_ref=halo_p.at[side],
                send_sem=hs_sem.at[2 + side],
                recv_sem=hr_sem.at[2 + side],
                device_id=to,
                device_id_type=MESH,
            ),
        )

    halos = halo(0, nxt_id) + halo(1, prv_id)
    for c in halos:
        c.start()

    up_re = jnp.dot(leaf[:, :128], imat[...], preferred_element_type=F)
    up_im = jnp.dot(leaf[:, 128:], imat[...], preferred_element_type=F)
    turns = phase[...] * (1.0 / (2.0 * math.pi))
    cosp = cos_turns(turns)
    sinp = cos_turns(turns - 0.25)
    for q in range(2):
        re = jnp.zeros((8, 512), F)
        im = jnp.zeros((8, 512), F)
        for c in range(8):
            at = 64 * q + 8 * c
            cc, sc = cosp[c : c + 1, :], sinp[c : c + 1, :]
            ur, ui = up_re[at : at + 8], up_im[at : at + 8]
            re = re + (cc * ur - sc * ui)
            im = im + (sc * ur + cc * ui)
        both = jnp.concatenate([re, im], axis=0).astype(BF)
        for a in range(4):
            stage[a, q] = both[:, 128 * a : 128 * a + 128]

    def tables(block, positions):
        p = [positions[k].astype(F) for k in range(3)]
        norm = (p[0] * p[0] + p[1] * p[1] + p[2] * p[2]) * (TURN * TURN)
        parts = three_parts(norm)
        one = jnp.ones_like(norm)
        for k in range(3):
            for j in range(3):
                rows32[3 * j + k, block] = p[k]
            rows32[9 + k, block] = one
            rows32[12 + k, block] = parts[k]
        rows32[15, block] = jnp.zeros_like(norm)
        if block == 1:
            for k in range(3):
                scaled = three_parts(p[k] * (-2.0 * TURN * TURN))
                for j in range(3):
                    own32[3 * j + k] = scaled[j]
                own32[9 + k] = parts[k]
                own32[12 + k] = one
            own32[15] = jnp.zeros_like(norm)

    def currents_of(block, values):
        for i in range(boxes // 2):
            pair = values[16 * i : 16 * i + 16].astype(F)
            for h in range(2):
                one_box = pair[8 * h : 8 * h + 8]
                x_tab[block * boxes + 2 * i + h] = jnp.concatenate(
                    [one_box, jnp.zeros_like(one_box)], axis=0
                ).astype(BF)

    tables(1, pos)
    currents_of(1, cur)

    def own_step(i, carry):
        own_tab[i] = own32[:, i, :].T.astype(BF)
        return carry

    lax.fori_loop(0, boxes, own_step, 0, unroll=4)

    def group(k):
        to = peer(k)
        return pltpu.make_async_remote_copy(
            src_ref=stage.at[lax.rem(to, 4)],
            dst_ref=window.at[pl.ds(2 * n_dir + 2 * d, 2)],
            send_sem=gs_sem.at[k],
            recv_sem=gr_sem.at[k],
            device_id=(box, to),
            device_id_type=MESH,
        )

    for k in range(1, n_dir):
        group(k).start()
    window[pl.ds(2 * n_dir + 2 * d, 2)] = stage[quarter]

    for c in halos:
        c.wait()
    for side in range(2):
        tables(2 * side, halo_p.at[side])
        currents_of(2 * side, halo_x.at[side])

    for block in range(3):

        def src_step(i, carry):
            src_tab[block * boxes + i] = rows32[:, block, i, :].astype(BF)
            return carry

        lax.fori_loop(0, boxes, src_step, 0, unroll=8)

    def spread(side, to):
        return pltpu.make_async_remote_copy(
            src_ref=window.at[pl.ds(2 * n_dir, 2 * n_dir)],
            dst_ref=window.at[pl.ds(4 * n_dir * side, 2 * n_dir)],
            send_sem=ss_sem.at[side],
            recv_sem=sr_sem.at[side],
            device_id=to,
            device_id_type=MESH,
        )

    def returned(k):
        to = 4 * fourth + lax.rem(quarter + k, 4)
        return pltpu.make_async_remote_copy(
            src_ref=loc.at[lax.rem(quarter + k, 4)],
            dst_ref=back.at[quarter],
            send_sem=bs_sem.at[k],
            recv_sem=br_sem.at[k],
            device_id=(box, to),
            device_id_type=MESH,
        )

    base = (me - 1) * boxes
    pairs = entries // 2

    def boxes_step(step, carry):
        @pl.when(step == SPREAD_AT)
        def _():
            for k in range(1, n_dir):
                group(k).wait()
            spread(0, up_id).start()
            spread(1, down_id).start()

        @pl.when(step == TRANSLATE_AT)
        def _():
            spread(0, up_id).wait()
            spread(1, down_id).wait()
            tab_copy.wait()
            tab[ops] = jnp.zeros((2, 128), F)
            group_base = (box - 1) * (2 * n_dir)

            def target(r, inner):
                line = 8 * fourth + r
                count = trans_count[line]
                re = jnp.zeros((8, 128), F)
                im = jnp.zeros((8, 128), F)
                for e in range(trans_entries):
                    at = inside(trans_src[line, e] - group_base, 6 * n_dir)
                    op = jnp.where(e < count, inside(trans_id[line, e], ops), ops)
                    src = window[at].astype(F)
                    co = tab[op]
                    cr, ci = co[0:1, :], co[1:2, :]
                    re = re + (cr * src[:8] - ci * src[8:])
                    im = im + (cr * src[8:] + ci * src[:8])
                loc[r // 2, lax.rem(r, 2)] = jnp.concatenate([re, im], axis=0).astype(BF)
                return inner

            lax.fori_loop(0, 8, target, 0)

        @pl.when(step == RETURN_AT)
        def _():
            for k in range(1, 4):
                returned(k).start()
            back[quarter] = loc[quarter]

        for h in range(2):
            i = 2 * step + h
            lhs = own_tab[i]
            acc = None
            for j in range(pairs + 1):
                if j < pairs:
                    s0 = inside(near_src[i, 2 * j] - base, 3 * boxes)
                    s1 = inside(near_src[i, 2 * j + 1] - base, 3 * boxes)
                    rhs = jnp.concatenate([src_tab[s0], src_tab[s1]], axis=1)
                    x = jnp.concatenate([x_tab[s0], x_tab[s1]], axis=1)
                else:
                    s0 = inside(near_src[i, 2 * pairs] - base, 3 * boxes)
                    rhs, x = src_tab[s0], x_tab[s0]
                tile = near_tile(jnp.dot(lhs, rhs, preferred_element_type=F))
                part = lax.dot_general(tile, x, NT_DIMS, preferred_element_type=F)
                acc = part if acc is None else acc + part
            near[i] = acc.T[:8]
        return carry

    lax.fori_loop(0, boxes // 2, boxes_step, 0)

    for k in range(1, 4):
        returned(k).wait()
    down_re, down_im = [], []
    for q in range(2):
        got = jnp.concatenate([back[a, q].astype(F) for a in range(4)], axis=1)
        lr, li = got[:8], got[8:]
        for c in range(8):
            cc, sc = cosp[c : c + 1, :], sinp[c : c + 1, :]
            down_re.append(cc * lr + sc * li)
            down_im.append(cc * li - sc * lr)
    in_re = lax.dot_general(
        jnp.concatenate(down_re, axis=0).astype(BF), imat[...], NT_DIMS, preferred_element_type=F
    )
    in_im = lax.dot_general(
        jnp.concatenate(down_im, axis=0).astype(BF), imat[...], NT_DIMS, preferred_element_type=F
    )
    incoming = jnp.concatenate([in_re, in_im], axis=1).astype(BF)
    far = lax.dot_general(incoming, rad[...], NT_DIMS, preferred_element_type=F)
    scale = 2.0 / math.sqrt(entries * 128)
    out[...] = near[...].reshape(boxes * 8, 128) * scale + far


def per_device(
    currents,
    positions,
    radiation,
    interp_index,
    interp_weight,
    child_phase,
    near_src,
    trans_src,
    trans_id,
    trans_count,
    trans_table,
):
    boxes, waves, width = currents.shape
    n_box, n_dir = lax.axis_size("box"), lax.axis_size("dir")
    ops = trans_table.shape[0]
    dims = (n_box, n_dir, boxes, near_src.shape[1], trans_src.shape[1], ops)
    smem = pl.BlockSpec(memory_space=pltpu.SMEM)
    vmem = pl.BlockSpec(memory_space=pltpu.VMEM)
    dma = pltpu.SemaphoreType.DMA
    field = pl.pallas_call(
        functools.partial(kernel, dims),
        out_shape=jax.ShapeDtypeStruct((boxes * waves, width), F),
        in_specs=[smem] * 4 + [vmem] * 6 + [pl.BlockSpec(memory_space=pl.ANY)],
        out_specs=vmem,
        scratch_shapes=[
            pltpu.VMEM((2, boxes * waves, width), BF),
            pltpu.VMEM((2, 3, boxes, width), BF),
            pltpu.VMEM((ops + 1, 2, 128), F),
            pltpu.VMEM((128, 512), BF),
            pltpu.VMEM((4, 2, 16, 128), BF),
            pltpu.VMEM((6 * n_dir, 16, 128), BF),
            pltpu.VMEM((4, 2, 16, 128), BF),
            pltpu.VMEM((4, 2, 16, 128), BF),
            pltpu.VMEM((16, 3, boxes, 128), F),
            pltpu.VMEM((16, boxes, 128), F),
            pltpu.VMEM((3 * boxes, 16, 128), BF),
            pltpu.VMEM((3 * boxes, 16, 128), BF),
            pltpu.VMEM((boxes, 128, 16), BF),
            pltpu.VMEM((boxes, 8, 128), F),
            dma,
            dma((4,)),
            dma((4,)),
            dma((16,)),
            dma((16,)),
            dma((2,)),
            dma((2,)),
            dma((4,)),
            dma((4,)),
        ],
        compiler_params=pltpu.CompilerParams(
            collective_id=0, has_side_effects=True, vmem_limit_bytes=48 * 1024 * 1024
        ),
        name="mlfma",
    )(
        near_src,
        trans_src,
        trans_id,
        trans_count,
        currents.reshape(boxes * waves, width),
        positions.transpose(1, 0, 2),
        radiation,
        interp_index.T,
        interp_weight.T,
        child_phase,
        trans_table,
    )
    return field.reshape(boxes, waves, width)


def solution(mesh):
    placed = (
        P(("box", "dir"), None, None),
        P(("box", "dir"), None, None),
        P(),
        P(),
        P(),
        P(),
        P(("box", "dir"), None),
        P("box", None),
        P("box", None),
        P("box"),
        P(),
    )
    return jax.shard_map(
        per_device,
        mesh=mesh,
        in_specs=placed,
        out_specs=P(("box", "dir"), None, None),
        check_vma=False,
    )
```

```python
import functools
import math

import jax
import jax.numpy as jnp
from jax import lax
from jax.experimental import pallas as pl
from jax.experimental.pallas import tpu as pltpu
from jax.sharding import PartitionSpec as P

F = jnp.float32
BF = jnp.bfloat16
MESH = pl.DeviceIdType.MESH
NT_DIMS = (((1,), (1,)), ((), ()))

TURN = 4.0 / (2.0 * math.pi)
SIN_TURN = (6.283164044284151, -41.33714236874864, 81.34076881229882, -70.99343258230081)
SIN_TURN_LONG = (
    6.283185160089382,
    -41.34165503139618,
    81.60100407210419,
    -76.54978226888187,
    39.536705889889106,
)
TINY = 2e-6

STRIDE = 4


def cos_turns(turns):
    z = 0.25 - jnp.abs(turns - jnp.round(turns))
    v = z * z
    acc = jnp.full_like(v, SIN_TURN_LONG[-1])
    for c in SIN_TURN_LONG[-2::-1]:
        acc = acc * v + c
    return acc * z


def near_tile(dist_sq):
    turns = dist_sq * lax.rsqrt(jnp.maximum(dist_sq, TINY))
    z = 0.25 - jnp.abs(turns - jnp.round(turns))
    ratio = (z / (turns + 0.5 * TURN)).astype(BF)
    v = z.astype(BF)
    v = v * v
    coefs = [jnp.asarray(c / math.pi, BF) for c in SIN_TURN]
    acc = v * coefs[-1] + coefs[-2]
    for c in coefs[-3::-1]:
        acc = acc * v + c
    return acc * ratio


def inside(index, size):
    return jnp.minimum(jnp.maximum(index, 0), size - 1)


def three_parts(x):
    high = x.astype(BF).astype(F)
    rest = x - high
    mid = rest.astype(BF).astype(F)
    return high, mid, rest - mid


def prepare_kernel(
    dims,
    cur_in,
    pos_in,
    rad_in,
    idx_in,
    wgt_in,
    phase_in,
    near_in,
    src_in,
    id_in,
    near_list,
    src_list,
    id_list,
    src_tab,
    x_tab,
    own_tab,
    stage,
    imat,
    cosp,
    sinp,
    cur,
    pos,
    rad,
    idx,
    wgt,
    phase,
    near_src,
    trans_src,
    trans_id,
    halo_x,
    halo_p,
    rows32,
    own32,
    in_sem,
    hs_sem,
    hr_sem,
):
    n_box, n_dir, boxes, ops = dims
    me = lax.axis_index("box") * n_dir + lax.axis_index("dir")
    n_dev = n_box * n_dir
    nxt = lax.rem(me + 1, n_dev)
    prv = lax.rem(me + n_dev - 1, n_dev)
    nxt_id = (nxt // n_dir, lax.rem(nxt, n_dir))
    prv_id = (prv // n_dir, lax.rem(prv, n_dir))

    has_nxt, has_prv = me < n_dev - 1, me > 0
    barrier = pltpu.get_barrier_semaphore()
    for has, to in ((has_nxt, nxt_id), (has_prv, prv_id)):

        @pl.when(has)
        def _():
            pl.semaphore_signal(barrier, inc=1, device_id=to, device_id_type=MESH)

    moves = [
        pltpu.make_async_copy(a, b, in_sem.at[k])
        for k, (a, b) in enumerate(
            [
                (cur_in, cur),
                (pos_in, pos),
                (idx_in, idx),
                (wgt_in, wgt),
                (rad_in, rad),
                (phase_in, phase),
                (near_in, near_src),
                (src_in, trans_src),
                (id_in, trans_id),
            ]
        )
    ]
    for m in moves:
        m.start()

    def halo(side, to):
        return (
            pltpu.make_async_remote_copy(
                src_ref=cur_in,
                dst_ref=halo_x.at[side],
                send_sem=hs_sem.at[side],
                recv_sem=hr_sem.at[side],
                device_id=to,
                device_id_type=MESH,
            ),
            pltpu.make_async_remote_copy(
                src_ref=pos_in,
                dst_ref=halo_p.at[side],
                send_sem=hs_sem.at[2 + side],
                recv_sem=hr_sem.at[2 + side],
                device_id=to,
                device_id_type=MESH,
            ),
        )

    pl.semaphore_wait(barrier, has_nxt.astype(jnp.int32) + has_prv.astype(jnp.int32))

    for side, has, to in ((0, has_nxt, nxt_id), (1, has_prv, prv_id)):

        @pl.when(has)
        def _():
            for c in halo(side, to):
                c.start()

    for m in moves:
        m.wait()
    near_list[...] = inside(near_src[...] - (me - 1) * boxes, 3 * boxes)
    group_base = (lax.axis_index("box") - 1) * (2 * n_dir)
    src_list[...] = inside(trans_src[...] - group_base, 6 * n_dir)
    id_list[...] = inside(trans_id[...], ops)
    row = lax.broadcasted_iota(jnp.int32, (128, 512), 0)
    acc = jnp.zeros((128, 512), F)
    for s in range(4):
        acc = acc + jnp.where(idx[s : s + 1, :] == row, wgt[s : s + 1, :], 0.0)
    imat[...] = acc.astype(BF)

    leaf = jnp.dot(cur[...], rad[...], preferred_element_type=F).astype(BF)
    up_re = jnp.dot(leaf[:, :128], imat[...], preferred_element_type=F)
    up_im = jnp.dot(leaf[:, 128:], imat[...], preferred_element_type=F)
    turns = phase[...] * (1.0 / (2.0 * math.pi))
    cosv = cos_turns(turns)
    sinv = cos_turns(turns - 0.25)
    cosp[...] = cosv
    sinp[...] = sinv
    for q in range(2):
        re = jnp.zeros((8, 512), F)
        im = jnp.zeros((8, 512), F)
        for c in range(8):
            at = 64 * q + 8 * c
            cc, sc = cosv[c : c + 1, :], sinv[c : c + 1, :]
            ur, ui = up_re[at : at + 8], up_im[at : at + 8]
            re = re + (cc * ur - sc * ui)
            im = im + (sc * ur + cc * ui)
        both = jnp.concatenate([re, im], axis=0).astype(BF)
        for a in range(4):
            stage[a, q] = both[:, 128 * a : 128 * a + 128]

    width = 3 * boxes

    def tables(block, positions):
        def put(k, value):
            rows32[k * width + block * boxes : k * width + (block + 1) * boxes] = value

        def put_own(k, value):
            own32[k * boxes : (k + 1) * boxes] = value

        p = [positions[k].astype(F) for k in range(3)]
        norm = (p[0] * p[0] + p[1] * p[1] + p[2] * p[2]) * (TURN * TURN)
        parts = three_parts(norm)
        one = jnp.ones_like(norm)
        for k in range(3):
            for j in range(3):
                put(3 * j + k, p[k])
            put(9 + k, one)
            put(12 + k, parts[k])
        put(15, jnp.zeros_like(norm))
        if block == 1:
            for k in range(3):
                scaled = three_parts(p[k] * (-2.0 * TURN * TURN))
                for j in range(3):
                    put_own(3 * j + k, scaled[j])
                put_own(9 + k, parts[k])
                put_own(12 + k, one)
            put_own(15, jnp.zeros_like(norm))
        for i in range(boxes):
            src_tab[block * boxes + i] = rows32[
                pl.ds(block * boxes + i, 16, stride=width), :
            ].astype(BF)

    def currents_of(block, values):
        for i in range(boxes // 2):
            pair = values[16 * i : 16 * i + 16].astype(F)
            for h in range(2):
                one_box = pair[8 * h : 8 * h + 8]
                x_tab[block * boxes + 2 * i + h] = jnp.concatenate(
                    [one_box, jnp.zeros_like(one_box)], axis=0
                ).astype(BF)

    tables(1, pos)
    currents_of(1, cur)
    for i in range(boxes):
        own_tab[i] = own32[pl.ds(i, 16, stride=boxes), :].T.astype(BF)

    for side, to_has, to, from_has in (
        (0, has_nxt, nxt_id, has_prv),
        (1, has_prv, prv_id, has_nxt),
    ):

        @pl.when(to_has)
        def _():
            for c in halo(side, to):
                c.wait_send()

        @pl.when(from_has)
        def _():
            for c in halo(side, to):
                c.wait_recv()

        @pl.when(jnp.logical_not(from_has))
        def _():
            halo_x[side] = jnp.zeros_like(halo_x[side])
            halo_p[side] = jnp.zeros_like(halo_p[side])

    for side in range(2):
        tables(2 * side, halo_p.at[side])
        currents_of(2 * side, halo_x.at[side])


def field_kernel(
    dims,
    near_list,
    src_list,
    id_list,
    src_tab,
    x_tab,
    own_tab,
    stage,
    imat,
    cosp,
    sinp,
    rad_in,
    count_in,
    table_in,
    out,
    rad,
    trans_src,
    trans_id,
    trans_count,
    tab,
    window,
    loc,
    back,
    near,
    ahead,
    in_sem,
    gs_sem,
    gr_sem,
    ss_sem,
    sr_sem,
    bs_sem,
    br_sem,
):
    n_box, n_dir, boxes, entries, trans_entries, ops = dims
    box = lax.axis_index("box")
    d = lax.axis_index("dir")
    quarter = lax.rem(d, 4)
    fourth = d // 4
    up_id = (lax.rem(box + 1, n_box), d)
    down_id = (lax.rem(box + n_box - 1, n_box), d)

    def peer(k):
        return lax.rem(d + k, n_dir)

    barrier = pltpu.get_barrier_semaphore()
    for to in (up_id, down_id):
        pl.semaphore_signal(barrier, inc=1, device_id=to, device_id_type=MESH)
    for k in range(1, n_dir):
        pl.semaphore_signal(barrier, inc=1, device_id=(box, peer(k)), device_id_type=MESH)

    lanes = pl.ds(pl.multiple_of(quarter * 128, 128), 128)
    moves = [
        pltpu.make_async_copy(a, b, in_sem.at[k])
        for k, (a, b) in enumerate(
            [
                (table_in.at[:, :, lanes], tab.at[pl.ds(0, ops)]),
                (src_list, trans_src),
                (id_list, trans_id),
                (count_in, trans_count),
                (rad_in, rad),
            ]
        )
    ]
    for m in moves:
        m.start()

    def group(k):
        to = peer(k)
        return pltpu.make_async_remote_copy(
            src_ref=stage.at[lax.rem(to, 4)],
            dst_ref=window.at[pl.ds(2 * n_dir + 2 * d, 2)],
            send_sem=gs_sem.at[k],
            recv_sem=gr_sem.at[k],
            device_id=(box, to),
            device_id_type=MESH,
        )

    def spread(side, to):
        return pltpu.make_async_remote_copy(
            src_ref=window.at[pl.ds(2 * n_dir, 2 * n_dir)],
            dst_ref=window.at[pl.ds(4 * n_dir * side, 2 * n_dir)],
            send_sem=ss_sem.at[side],
            recv_sem=sr_sem.at[side],
            device_id=to,
            device_id_type=MESH,
        )

    def returned(k):
        to = lax.rem(quarter + k, 4)
        return pltpu.make_async_remote_copy(
            src_ref=loc.at[to],
            dst_ref=back.at[quarter],
            send_sem=bs_sem.at[k],
            recv_sem=br_sem.at[k],
            device_id=(box, 4 * fourth + to),
            device_id_type=MESH,
        )

    def gather_start():
        pl.semaphore_wait(barrier, n_dir + 1)
        for k in range(1, n_dir):
            group(k).start()
        window[pl.ds(2 * n_dir + 2 * d, 2)] = stage[quarter]

    def spread_start():
        for k in range(1, n_dir):
            group(k).wait()
        spread(0, up_id).start()
        spread(1, down_id).start()

    def translate():
        spread(0, up_id).wait()
        spread(1, down_id).wait()
        for m in moves:
            m.wait()
        tab[ops] = jnp.zeros((2, 128), F)

        def target(r, inner):
            to = lax.rem(quarter + 1 + r // 2, 4)
            line = 8 * fourth + 2 * to + lax.rem(r, 2)
            count = trans_count[line]
            re = jnp.zeros((8, 128), F)
            im = jnp.zeros((8, 128), F)
            for e in range(trans_entries):
                op = jnp.where(e < count, trans_id[line, e], ops)
                src = window[trans_src[line, e]].astype(F)
                co = tab[op]
                cr, ci = co[0:1, :], co[1:2, :]
                re = re + (cr * src[:8] - ci * src[8:])
                im = im + (cr * src[8:] + ci * src[:8])
            loc[to, lax.rem(r, 2)] = jnp.concatenate([re, im], axis=0).astype(BF)
            return inner

        lax.fori_loop(0, 8, target, 0)
        for k in range(1, 4):
            returned(k).start()
        back[quarter] = loc[quarter]

    pairs = entries // 2

    def sources(i, j):
        return [near_list[i, e] for e in range(2 * j, min(2 * j + 2, entries))]

    def joined(ref, i, j):
        parts = [ref[s] for s in sources(i, j)]
        return jnp.concatenate(parts, axis=1) if len(parts) > 1 else parts[0]

    def distances(i, j):
        return jnp.dot(own_tab[i], joined(src_tab, i, j), preferred_element_type=F)

    steps = boxes // STRIDE
    first_half = jnp.logical_and(d >= 2, d < n_dir // 2)
    gather_at = jnp.where(jnp.logical_and(d >= 2, d < 3 * n_dir // 8), 2, 1)
    spread_at = jnp.where(first_half, 3, 2)
    translate_at = jnp.where(first_half, steps, 3)

    def boxes_step(step, carry):
        pl.when(step == gather_at)(gather_start)
        pl.when(step == spread_at)(spread_start)
        pl.when(step == translate_at)(translate)
        tasks = [(STRIDE * step + h, j) for h in range(STRIDE) for j in range(pairs + 1)]
        later = (jnp.minimum(STRIDE * (step + 1), boxes - 1), 0)
        dist = ahead[...]
        acc = None
        for t, (i, j) in enumerate(tasks):
            if t + 1 < len(tasks):
                dist_next = distances(*tasks[t + 1])
            else:
                ahead[...] = distances(*later)
            tile = near_tile(dist)
            part = lax.dot_general(tile, joined(x_tab, i, j), NT_DIMS, preferred_element_type=F)
            acc = part if acc is None else acc + part
            if j == pairs:
                near[i] = acc.T[:8]
                acc = None
            dist = dist_next
        return carry

    ahead[...] = distances(0, 0)
    lax.fori_loop(0, steps, boxes_step, 0)
    pl.when(translate_at == steps)(translate)

    for k in range(1, 4):
        returned(k).wait()
    down_re, down_im = [], []
    for q in range(2):
        got = jnp.concatenate([back[a, q].astype(F) for a in range(4)], axis=1)
        lr, li = got[:8], got[8:]
        for c in range(8):
            cc, sc = cosp[c : c + 1, :], sinp[c : c + 1, :]
            down_re.append(cc * lr + sc * li)
            down_im.append(cc * li - sc * lr)
    in_re = lax.dot_general(
        jnp.concatenate(down_re, axis=0).astype(BF), imat[...], NT_DIMS, preferred_element_type=F
    )
    in_im = lax.dot_general(
        jnp.concatenate(down_im, axis=0).astype(BF), imat[...], NT_DIMS, preferred_element_type=F
    )
    incoming = jnp.concatenate([in_re, in_im], axis=1).astype(BF)
    far = lax.dot_general(incoming, rad[...], NT_DIMS, preferred_element_type=F)
    scale = 2.0 / math.sqrt(entries * 128)
    out[...] = near[...].reshape(boxes * 8, 128) * scale + far


def in_hbm(x):
    return pltpu.with_memory_space_constraint(x, pltpu.HBM)


def per_device(
    currents,
    positions,
    radiation,
    interp_index,
    interp_weight,
    child_phase,
    near_src,
    trans_src,
    trans_id,
    trans_count,
    trans_table,
):
    boxes, waves, width = currents.shape
    n_box, n_dir = lax.axis_size("box"), lax.axis_size("dir")
    ops = trans_table.shape[0]
    smem = pl.BlockSpec(memory_space=pltpu.SMEM)
    vmem = pl.BlockSpec(memory_space=pltpu.VMEM)
    hbm = pl.BlockSpec(memory_space=pltpu.HBM)
    dma = pltpu.SemaphoreType.DMA
    shape = jax.ShapeDtypeStruct
    cur = currents.reshape(boxes * waves, width)
    pos = positions.transpose(1, 0, 2)
    idx = interp_index.T
    wgt = interp_weight.T
    prepared = pl.pallas_call(
        functools.partial(prepare_kernel, (n_box, n_dir, boxes, ops)),
        out_shape=[
            shape(near_src.shape, jnp.int32),
            shape(trans_src.shape, jnp.int32),
            shape(trans_id.shape, jnp.int32),
            shape((3 * boxes, 16, 128), BF),
            shape((3 * boxes, 16, 128), BF),
            shape((boxes, 128, 16), BF),
            shape((4, 2, 16, 128), BF),
            shape((128, 512), BF),
            shape((8, 512), F),
            shape((8, 512), F),
        ],
        in_specs=[hbm] * 9,
        out_specs=[vmem] * 10,
        scratch_shapes=[
            pltpu.VMEM(cur.shape, BF),
            pltpu.VMEM(pos.shape, BF),
            pltpu.VMEM(radiation.shape, BF),
            pltpu.VMEM(idx.shape, jnp.int32),
            pltpu.VMEM(wgt.shape, F),
            pltpu.VMEM(child_phase.shape, F),
            pltpu.VMEM(near_src.shape, jnp.int32),
            pltpu.VMEM(trans_src.shape, jnp.int32),
            pltpu.VMEM(trans_id.shape, jnp.int32),
            pltpu.VMEM((2,) + cur.shape, BF),
            pltpu.VMEM((2,) + pos.shape, BF),
            pltpu.VMEM((16 * 3 * boxes, 128), F),
            pltpu.VMEM((16 * boxes, 128), F),
            dma((9,)),
            dma((4,)),
            dma((4,)),
        ],
        compiler_params=pltpu.CompilerParams(
            collective_id=0, has_side_effects=True, vmem_limit_bytes=16 * 1024 * 1024
        ),
        name="prepare",
    )(
        *map(
            in_hbm,
            (cur, pos, radiation, idx, wgt, child_phase, near_src, trans_src, trans_id),
        )
    )
    dims = (n_box, n_dir, boxes, near_src.shape[1], trans_src.shape[1], ops)
    field = pl.pallas_call(
        functools.partial(field_kernel, dims),
        out_shape=shape((boxes * waves, width), F),
        in_specs=[smem] + [vmem] * 9 + [hbm] * 3,
        out_specs=vmem,
        scratch_shapes=[
            pltpu.VMEM(radiation.shape, BF),
            pltpu.SMEM(trans_src.shape, jnp.int32),
            pltpu.SMEM(trans_id.shape, jnp.int32),
            pltpu.SMEM(trans_count.shape, jnp.int32),
            pltpu.VMEM((ops + 1, 2, 128), F),
            pltpu.VMEM((6 * n_dir, 16, 128), BF),
            pltpu.VMEM((4, 2, 16, 128), BF),
            pltpu.VMEM((4, 2, 16, 128), BF),
            pltpu.VMEM((boxes, 8, 128), F),
            pltpu.VMEM((128, 256), F),
            dma((5,)),
            dma((16,)),
            dma((16,)),
            dma((2,)),
            dma((2,)),
            dma((4,)),
            dma((4,)),
        ],
        compiler_params=pltpu.CompilerParams(
            collective_id=1, has_side_effects=True, vmem_limit_bytes=32 * 1024 * 1024
        ),
        name="field",
    )(*prepared, *map(in_hbm, (radiation, trans_count, trans_table)))
    return field.reshape(boxes, waves, width)


def solution(mesh):
    placed = (
        P(("box", "dir"), None, None),
        P(("box", "dir"), None, None),
        P(),
        P(),
        P(),
        P(),
        P(("box", "dir"), None),
        P("box", None),
        P("box", None),
        P("box"),
        P(),
    )
    return jax.shard_map(
        per_device,
        mesh=mesh,
        in_specs=placed,
        out_specs=P(("box", "dir"), None, None),
        check_vma=False,
    )
```

```python
import functools
import math

import jax
import jax.numpy as jnp
from jax import lax
from jax.experimental import pallas as pl
from jax.experimental.pallas import tpu as pltpu
from jax.sharding import PartitionSpec as P

F = jnp.float32
BF = jnp.bfloat16
MESH = pl.DeviceIdType.MESH
NT_DIMS = (((1,), (1,)), ((), ()))

TURN = 4.0 / (2.0 * math.pi)
SIN_TURN = (6.283164044284151, -41.33714236874864, 81.34076881229882, -70.99343258230081)
SIN_TURN_LONG = (
    6.283185160089382,
    -41.34165503139618,
    81.60100407210419,
    -76.54978226888187,
    39.536705889889106,
)
TINY = 2e-6

STRIDE = 4


def cos_turns(turns):
    z = 0.25 - jnp.abs(turns - jnp.round(turns))
    v = z * z
    acc = jnp.full_like(v, SIN_TURN_LONG[-1])
    for c in SIN_TURN_LONG[-2::-1]:
        acc = acc * v + c
    return acc * z


def near_tile(dist_sq):
    turns = dist_sq * lax.rsqrt(jnp.maximum(dist_sq, TINY))
    z = 0.25 - jnp.abs(turns - jnp.round(turns))
    ratio = (z / (turns + 0.5 * TURN)).astype(BF)
    v = z.astype(BF)
    v = v * v
    coefs = [jnp.asarray(c / math.pi, BF) for c in SIN_TURN]
    acc = v * coefs[-1] + coefs[-2]
    for c in coefs[-3::-1]:
        acc = acc * v + c
    return acc * ratio


def inside(index, size):
    return jnp.minimum(jnp.maximum(index, 0), size - 1)


def distances(own, sources):
    rows = jnp.concatenate(sources, axis=1) if len(sources) > 1 else sources[0]
    return jnp.dot(own.astype(BF), rows.astype(BF), preferred_element_type=F)


def applied(tile, currents):
    rows = jnp.concatenate(currents, axis=1) if len(currents) > 1 else currents[0]
    rows = jnp.concatenate([rows, jnp.zeros_like(rows)], axis=0).astype(BF)
    return lax.dot_general(tile, rows, NT_DIMS, preferred_element_type=F)


def three_parts(x):
    high = x.astype(BF).astype(F)
    rest = x - high
    mid = rest.astype(BF).astype(F)
    return high, mid, rest - mid


def prepare_kernel(
    dims,
    cur_in,
    pos_in,
    rad_in,
    idx_in,
    wgt_in,
    phase_in,
    near_in,
    src_in,
    id_in,
    near_list,
    src_list,
    id_list,
    src_tab,
    x_tab,
    own_tab,
    near_self,
    stage,
    imat,
    cosp,
    sinp,
    cur,
    pos,
    rad,
    idx,
    wgt,
    phase,
    near_src,
    trans_src,
    trans_id,
    halo_x,
    halo_p,
    rows32,
    own32,
    in_sem,
    hs_sem,
    hr_sem,
):
    n_box, n_dir, boxes, ops = dims
    me = lax.axis_index("box") * n_dir + lax.axis_index("dir")
    n_dev = n_box * n_dir
    nxt = lax.rem(me + 1, n_dev)
    prv = lax.rem(me + n_dev - 1, n_dev)
    nxt_id = (nxt // n_dir, lax.rem(nxt, n_dir))
    prv_id = (prv // n_dir, lax.rem(prv, n_dir))

    has_nxt, has_prv = me < n_dev - 1, me > 0
    barrier = pltpu.get_barrier_semaphore()
    for has, to in ((has_nxt, nxt_id), (has_prv, prv_id)):

        @pl.when(has)
        def _():
            pl.semaphore_signal(barrier, inc=1, device_id=to, device_id_type=MESH)

    moves = [
        pltpu.make_async_copy(a, b, in_sem.at[k])
        for k, (a, b) in enumerate(
            [
                (cur_in, cur),
                (pos_in, pos),
                (idx_in, idx),
                (wgt_in, wgt),
                (rad_in, rad),
                (phase_in, phase),
                (near_in, near_src),
                (src_in, trans_src),
                (id_in, trans_id),
            ]
        )
    ]
    for m in moves:
        m.start()

    def halo(side, to):
        return (
            pltpu.make_async_remote_copy(
                src_ref=cur_in,
                dst_ref=halo_x.at[side],
                send_sem=hs_sem.at[side],
                recv_sem=hr_sem.at[side],
                device_id=to,
                device_id_type=MESH,
            ),
            pltpu.make_async_remote_copy(
                src_ref=pos_in,
                dst_ref=halo_p.at[side],
                send_sem=hs_sem.at[2 + side],
                recv_sem=hr_sem.at[2 + side],
                device_id=to,
                device_id_type=MESH,
            ),
        )

    pl.semaphore_wait(barrier, has_nxt.astype(jnp.int32) + has_prv.astype(jnp.int32))

    for side, has, to in ((0, has_nxt, nxt_id), (1, has_prv, prv_id)):

        @pl.when(has)
        def _():
            for c in halo(side, to):
                c.start()

    for m in moves:
        m.wait()
    near_list[...] = inside(near_src[...] - (me - 1) * boxes, 3 * boxes)
    group_base = (lax.axis_index("box") - 1) * (2 * n_dir)
    src_list[...] = inside(trans_src[...] - group_base, 6 * n_dir)
    id_list[...] = inside(trans_id[...], ops)
    row = lax.broadcasted_iota(jnp.int32, (128, 512), 0)
    acc = jnp.zeros((128, 512), F)
    for s in range(4):
        acc = acc + jnp.where(idx[s : s + 1, :] == row, wgt[s : s + 1, :], 0.0)
    imat[...] = acc.astype(BF)

    leaf = jnp.dot(cur[...], rad[...], preferred_element_type=F).astype(BF)
    up_re = jnp.dot(leaf[:, :128], imat[...], preferred_element_type=F)
    up_im = jnp.dot(leaf[:, 128:], imat[...], preferred_element_type=F)
    turns = phase[...] * (1.0 / (2.0 * math.pi))
    cosv = cos_turns(turns)
    sinv = cos_turns(turns - 0.25)
    cosp[...] = cosv
    sinp[...] = sinv
    for q in range(2):
        re = jnp.zeros((8, 512), F)
        im = jnp.zeros((8, 512), F)
        for c in range(8):
            at = 64 * q + 8 * c
            cc, sc = cosv[c : c + 1, :], sinv[c : c + 1, :]
            ur, ui = up_re[at : at + 8], up_im[at : at + 8]
            re = re + (cc * ur - sc * ui)
            im = im + (sc * ur + cc * ui)
        both = jnp.concatenate([re, im], axis=0).astype(BF)
        for a in range(4):
            stage[a, q] = both[:, 128 * a : 128 * a + 128]

    width = 3 * boxes

    def tables(block, positions):
        def put(k, value):
            rows32[k * width + block * boxes : k * width + (block + 1) * boxes] = value

        def put_own(k, value):
            own32[k * boxes : (k + 1) * boxes] = value

        p = [positions[k].astype(F) for k in range(3)]
        norm = (p[0] * p[0] + p[1] * p[1] + p[2] * p[2]) * (TURN * TURN)
        parts = three_parts(norm)
        one = jnp.ones_like(norm)
        for k in range(3):
            for j in range(3):
                put(3 * j + k, p[k])
            put(9 + k, one)
            put(12 + k, parts[k])
        put(15, jnp.zeros_like(norm))
        if block == 1:
            for k in range(3):
                scaled = three_parts(p[k] * (-2.0 * TURN * TURN))
                for j in range(3):
                    put_own(3 * j + k, scaled[j])
                put_own(9 + k, parts[k])
                put_own(12 + k, one)
            put_own(15, jnp.zeros_like(norm))
        for i in range(boxes):
            src_tab[block * boxes + i] = rows32[pl.ds(block * boxes + i, 16, stride=width), :]

    def currents_of(block, values):
        for i in range(boxes // 2):
            pair = values[16 * i : 16 * i + 16].astype(F)
            for h in range(2):
                x_tab[block * boxes + 2 * i + h] = pair[8 * h : 8 * h + 8]

    tables(1, pos)
    currents_of(1, cur)
    for i in range(boxes):
        own_tab[i] = own32[pl.ds(i, 16, stride=boxes), :].T

    for i in range(boxes):
        tile = near_tile(distances(own_tab[i], [src_tab[boxes + i]]))
        near_self[i] = applied(tile, [x_tab[boxes + i]]).T[:8]

    for side, to_has, to, from_has in (
        (0, has_nxt, nxt_id, has_prv),
        (1, has_prv, prv_id, has_nxt),
    ):

        @pl.when(to_has)
        def _():
            for c in halo(side, to):
                c.wait_send()

        @pl.when(from_has)
        def _():
            for c in halo(side, to):
                c.wait_recv()

        @pl.when(jnp.logical_not(from_has))
        def _():
            halo_x[side] = jnp.zeros_like(halo_x[side])
            halo_p[side] = jnp.zeros_like(halo_p[side])

    for side in range(2):
        tables(2 * side, halo_p.at[side])
        currents_of(2 * side, halo_x.at[side])


def field_kernel(
    dims,
    near_list,
    src_list,
    id_list,
    src_tab,
    x_tab,
    own_tab,
    near_self,
    stage,
    imat,
    cosp,
    sinp,
    rad_in,
    count_in,
    table_in,
    out,
    rad,
    trans_src,
    trans_id,
    trans_count,
    tab,
    window,
    loc,
    back,
    near,
    ahead,
    in_sem,
    gs_sem,
    gr_sem,
    ss_sem,
    sr_sem,
    bs_sem,
    br_sem,
):
    n_box, n_dir, boxes, entries, trans_entries, ops = dims
    box = lax.axis_index("box")
    d = lax.axis_index("dir")
    quarter = lax.rem(d, 4)
    fourth = d // 4
    up_id = (lax.rem(box + 1, n_box), d)
    down_id = (lax.rem(box + n_box - 1, n_box), d)

    def peer(k):
        return lax.rem(d + k, n_dir)

    barrier = pltpu.get_barrier_semaphore()
    for to in (up_id, down_id):
        pl.semaphore_signal(barrier, inc=1, device_id=to, device_id_type=MESH)
    for k in range(1, n_dir):
        pl.semaphore_signal(barrier, inc=1, device_id=(box, peer(k)), device_id_type=MESH)

    lanes = pl.ds(pl.multiple_of(quarter * 128, 128), 128)
    moves = [
        pltpu.make_async_copy(a, b, in_sem.at[k])
        for k, (a, b) in enumerate(
            [
                (table_in.at[:, :, lanes], tab.at[pl.ds(0, ops)]),
                (src_list, trans_src),
                (id_list, trans_id),
                (count_in, trans_count),
                (rad_in, rad),
            ]
        )
    ]
    for m in moves:
        m.start()

    def group(k):
        to = peer(k)
        return pltpu.make_async_remote_copy(
            src_ref=stage.at[lax.rem(to, 4)],
            dst_ref=window.at[pl.ds(2 * n_dir + 2 * d, 2)],
            send_sem=gs_sem.at[k],
            recv_sem=gr_sem.at[k],
            device_id=(box, to),
            device_id_type=MESH,
        )

    def spread(side, to):
        return pltpu.make_async_remote_copy(
            src_ref=window.at[pl.ds(2 * n_dir, 2 * n_dir)],
            dst_ref=window.at[pl.ds(4 * n_dir * side, 2 * n_dir)],
            send_sem=ss_sem.at[side],
            recv_sem=sr_sem.at[side],
            device_id=to,
            device_id_type=MESH,
        )

    def returned(k):
        to = lax.rem(quarter + k, 4)
        return pltpu.make_async_remote_copy(
            src_ref=loc.at[to],
            dst_ref=back.at[quarter],
            send_sem=bs_sem.at[k],
            recv_sem=br_sem.at[k],
            device_id=(box, 4 * fourth + to),
            device_id_type=MESH,
        )

    def gather_start():
        pl.semaphore_wait(barrier, n_dir + 1)
        for k in range(1, n_dir):
            group(k).start()
        window[pl.ds(2 * n_dir + 2 * d, 2)] = stage[quarter]

    def spread_start():
        for k in range(1, n_dir):
            group(k).wait()
        spread(0, up_id).start()
        spread(1, down_id).start()

    def translate():
        spread(0, up_id).wait()
        spread(1, down_id).wait()
        for m in moves:
            m.wait()
        tab[ops] = jnp.zeros((2, 128), F)

        def target(r, inner):
            to = lax.rem(quarter + 1 + r // 2, 4)
            line = 8 * fourth + 2 * to + lax.rem(r, 2)
            count = trans_count[line]
            re = jnp.zeros((8, 128), F)
            im = jnp.zeros((8, 128), F)
            for e in range(trans_entries):
                op = jnp.where(e < count, trans_id[line, e], ops)
                src = window[trans_src[line, e]].astype(F)
                co = tab[op]
                cr, ci = co[0:1, :], co[1:2, :]
                re = re + (cr * src[:8] - ci * src[8:])
                im = im + (cr * src[8:] + ci * src[:8])
            loc[to, lax.rem(r, 2)] = jnp.concatenate([re, im], axis=0).astype(BF)
            return inner

        lax.fori_loop(0, 8, target, 0)
        for k in range(1, 4):
            returned(k).start()
        back[quarter] = loc[quarter]

    pairs = entries // 2

    def listed(ref, i, j):
        return [ref[near_list[i, e]] for e in range(2 * j + 1, min(2 * j + 3, entries))]

    def pair_distances(i, j):
        return distances(own_tab[i], listed(src_tab, i, j))

    steps = boxes // STRIDE
    first_half = jnp.logical_and(d >= 2, d < n_dir // 2)
    gather_at = jnp.where(jnp.logical_and(d >= 2, d < 3 * n_dir // 8), 2, 1)
    spread_at = jnp.where(first_half, 3, 2)
    translate_at = jnp.where(first_half, steps, 3)

    def boxes_step(step, carry):
        pl.when(step == gather_at)(gather_start)
        pl.when(step == spread_at)(spread_start)
        pl.when(step == translate_at)(translate)
        tasks = [(STRIDE * step + h, j) for h in range(STRIDE) for j in range(pairs)]
        later = (jnp.minimum(STRIDE * (step + 1), boxes - 1), 0)
        dist = ahead[...]
        acc = None
        for t, (i, j) in enumerate(tasks):
            if t + 1 < len(tasks):
                dist_next = pair_distances(*tasks[t + 1])
            else:
                ahead[...] = pair_distances(*later)
            part = applied(near_tile(dist), listed(x_tab, i, j))
            acc = part if acc is None else acc + part
            if j == pairs - 1:
                near[i] = acc.T[:8]
                acc = None
            dist = dist_next
        return carry

    ahead[...] = pair_distances(0, 0)
    lax.fori_loop(0, steps, boxes_step, 0)
    pl.when(translate_at == steps)(translate)

    for k in range(1, 4):
        returned(k).wait()
    down_re, down_im = [], []
    for q in range(2):
        got = jnp.concatenate([back[a, q].astype(F) for a in range(4)], axis=1)
        lr, li = got[:8], got[8:]
        for c in range(8):
            cc, sc = cosp[c : c + 1, :], sinp[c : c + 1, :]
            down_re.append(cc * lr + sc * li)
            down_im.append(cc * li - sc * lr)
    in_re = lax.dot_general(
        jnp.concatenate(down_re, axis=0).astype(BF), imat[...], NT_DIMS, preferred_element_type=F
    )
    in_im = lax.dot_general(
        jnp.concatenate(down_im, axis=0).astype(BF), imat[...], NT_DIMS, preferred_element_type=F
    )
    incoming = jnp.concatenate([in_re, in_im], axis=1).astype(BF)
    far = lax.dot_general(incoming, rad[...], NT_DIMS, preferred_element_type=F)
    scale = 2.0 / math.sqrt(entries * 128)
    out[...] = (near[...] + near_self[...]).reshape(boxes * 8, 128) * scale + far


def in_hbm(x):
    return pltpu.with_memory_space_constraint(x, pltpu.HBM)


def per_device(
    currents,
    positions,
    radiation,
    interp_index,
    interp_weight,
    child_phase,
    near_src,
    trans_src,
    trans_id,
    trans_count,
    trans_table,
):
    boxes, waves, width = currents.shape
    n_box, n_dir = lax.axis_size("box"), lax.axis_size("dir")
    ops = trans_table.shape[0]
    smem = pl.BlockSpec(memory_space=pltpu.SMEM)
    vmem = pl.BlockSpec(memory_space=pltpu.VMEM)
    hbm = pl.BlockSpec(memory_space=pltpu.HBM)
    dma = pltpu.SemaphoreType.DMA
    shape = jax.ShapeDtypeStruct
    cur = currents.reshape(boxes * waves, width)
    pos = positions.transpose(1, 0, 2)
    idx = interp_index.T
    wgt = interp_weight.T
    prepared = pl.pallas_call(
        functools.partial(prepare_kernel, (n_box, n_dir, boxes, ops)),
        out_shape=[
            shape(near_src.shape, jnp.int32),
            shape(trans_src.shape, jnp.int32),
            shape(trans_id.shape, jnp.int32),
            shape((3 * boxes, 16, 128), F),
            shape((3 * boxes, 8, 128), F),
            shape((boxes, 128, 16), F),
            shape((boxes, 8, 128), F),
            shape((4, 2, 16, 128), BF),
            shape((128, 512), BF),
            shape((8, 512), F),
            shape((8, 512), F),
        ],
        in_specs=[hbm] * 9,
        out_specs=[vmem] * 11,
        scratch_shapes=[
            pltpu.VMEM(cur.shape, BF),
            pltpu.VMEM(pos.shape, BF),
            pltpu.VMEM(radiation.shape, BF),
            pltpu.VMEM(idx.shape, jnp.int32),
            pltpu.VMEM(wgt.shape, F),
            pltpu.VMEM(child_phase.shape, F),
            pltpu.VMEM(near_src.shape, jnp.int32),
            pltpu.VMEM(trans_src.shape, jnp.int32),
            pltpu.VMEM(trans_id.shape, jnp.int32),
            pltpu.VMEM((2,) + cur.shape, BF),
            pltpu.VMEM((2,) + pos.shape, BF),
            pltpu.VMEM((16 * 3 * boxes, 128), F),
            pltpu.VMEM((16 * boxes, 128), F),
            dma((9,)),
            dma((4,)),
            dma((4,)),
        ],
        compiler_params=pltpu.CompilerParams(
            collective_id=0, has_side_effects=True, vmem_limit_bytes=16 * 1024 * 1024
        ),
        name="prepare",
    )(
        *map(
            in_hbm,
            (cur, pos, radiation, idx, wgt, child_phase, near_src, trans_src, trans_id),
        )
    )
    dims = (n_box, n_dir, boxes, near_src.shape[1], trans_src.shape[1], ops)
    field = pl.pallas_call(
        functools.partial(field_kernel, dims),
        out_shape=shape((boxes * waves, width), F),
        in_specs=[smem] + [vmem] * 10 + [hbm] * 3,
        out_specs=vmem,
        scratch_shapes=[
            pltpu.VMEM(radiation.shape, BF),
            pltpu.SMEM(trans_src.shape, jnp.int32),
            pltpu.SMEM(trans_id.shape, jnp.int32),
            pltpu.SMEM(trans_count.shape, jnp.int32),
            pltpu.VMEM((ops + 1, 2, 128), F),
            pltpu.VMEM((6 * n_dir, 16, 128), BF),
            pltpu.VMEM((4, 2, 16, 128), BF),
            pltpu.VMEM((4, 2, 16, 128), BF),
            pltpu.VMEM((boxes, 8, 128), F),
            pltpu.VMEM((128, 256), F),
            dma((5,)),
            dma((16,)),
            dma((16,)),
            dma((2,)),
            dma((2,)),
            dma((4,)),
            dma((4,)),
        ],
        compiler_params=pltpu.CompilerParams(
            collective_id=1, has_side_effects=True, vmem_limit_bytes=32 * 1024 * 1024
        ),
        name="field",
    )(*prepared, *map(in_hbm, (radiation, trans_count, trans_table)))
    return field.reshape(boxes, waves, width)


def solution(mesh):
    placed = (
        P(("box", "dir"), None, None),
        P(("box", "dir"), None, None),
        P(),
        P(),
        P(),
        P(),
        P(("box", "dir"), None),
        P("box", None),
        P("box", None),
        P("box"),
        P(),
    )
    return jax.shard_map(
        per_device,
        mesh=mesh,
        in_specs=placed,
        out_specs=P(("box", "dir"), None, None),
        check_vma=False,
    )
```

```python
import functools
import math

import jax
import jax.numpy as jnp
from jax import lax
from jax.experimental import pallas as pl
from jax.experimental.pallas import tpu as pltpu
from jax.sharding import PartitionSpec as P

F = jnp.float32
BF = jnp.bfloat16
MESH = pl.DeviceIdType.MESH
NT_DIMS = (((1,), (1,)), ((), ()))

TURN = 4.0 / (2.0 * math.pi)
SIN_TURN = (6.283164044284151, -41.33714236874864, 81.34076881229882, -70.99343258230081)
SIN_TURN_LONG = (
    6.283185160089382,
    -41.34165503139618,
    81.60100407210419,
    -76.54978226888187,
    39.536705889889106,
)
TINY = 2e-6

STRIDE = 2


def cos_turns(turns):
    z = 0.25 - jnp.abs(turns - jnp.round(turns))
    v = z * z
    acc = jnp.full_like(v, SIN_TURN_LONG[-1])
    for c in SIN_TURN_LONG[-2::-1]:
        acc = acc * v + c
    return acc * z


def near_tile(dist_sq):
    turns = dist_sq * lax.rsqrt(jnp.maximum(dist_sq, TINY))
    z = 0.25 - jnp.abs(turns - jnp.round(turns))
    ratio = (z / (turns + 0.5 * TURN)).astype(BF)
    v = z.astype(BF)
    v = v * v
    coefs = [jnp.asarray(c / math.pi, BF) for c in SIN_TURN]
    acc = v * coefs[-1] + coefs[-2]
    for c in coefs[-3::-1]:
        acc = acc * v + c
    return acc * ratio


def inside(index, size):
    return jnp.minimum(jnp.maximum(index, 0), size - 1)


def distances(own, sources):
    rows = jnp.concatenate(sources, axis=1) if len(sources) > 1 else sources[0]
    return jnp.dot(own.astype(BF), rows.astype(BF), preferred_element_type=F)


def applied(tile, currents):
    rows = jnp.concatenate(currents, axis=1) if len(currents) > 1 else currents[0]
    rows = jnp.concatenate([rows, jnp.zeros_like(rows)], axis=0).astype(BF)
    return lax.dot_general(tile, rows, NT_DIMS, preferred_element_type=F)


def three_parts(x):
    high = x.astype(BF).astype(F)
    rest = x - high
    mid = rest.astype(BF).astype(F)
    return high, mid, rest - mid


def prepare_kernel(
    dims,
    cur_in,
    pos_in,
    rad_in,
    idx_in,
    wgt_in,
    phase_in,
    near_in,
    src_in,
    id_in,
    near_list,
    src_list,
    id_list,
    src_tab,
    x_tab,
    own_tab,
    near_self,
    stage,
    imat,
    cosp,
    sinp,
    cur,
    pos,
    rad,
    idx,
    wgt,
    phase,
    near_src,
    trans_src,
    trans_id,
    halo_x,
    halo_p,
    rows32,
    own32,
    in_sem,
    hs_sem,
    hr_sem,
):
    n_box, n_dir, boxes, ops = dims
    me = lax.axis_index("box") * n_dir + lax.axis_index("dir")
    n_dev = n_box * n_dir
    nxt = lax.rem(me + 1, n_dev)
    prv = lax.rem(me + n_dev - 1, n_dev)
    nxt_id = (nxt // n_dir, lax.rem(nxt, n_dir))
    prv_id = (prv // n_dir, lax.rem(prv, n_dir))

    has_nxt, has_prv = me < n_dev - 1, me > 0
    barrier = pltpu.get_barrier_semaphore()
    for has, to in ((has_nxt, nxt_id), (has_prv, prv_id)):

        @pl.when(has)
        def _():
            pl.semaphore_signal(barrier, inc=1, device_id=to, device_id_type=MESH)

    moves = [
        pltpu.make_async_copy(a, b, in_sem.at[k])
        for k, (a, b) in enumerate(
            [
                (cur_in, cur),
                (pos_in, pos),
                (idx_in, idx),
                (wgt_in, wgt),
                (rad_in, rad),
                (phase_in, phase),
                (near_in, near_src),
                (src_in, trans_src),
                (id_in, trans_id),
            ]
        )
    ]
    for m in moves:
        m.start()

    def halo(side, to):
        return (
            pltpu.make_async_remote_copy(
                src_ref=cur_in,
                dst_ref=halo_x.at[side],
                send_sem=hs_sem.at[side],
                recv_sem=hr_sem.at[side],
                device_id=to,
                device_id_type=MESH,
            ),
            pltpu.make_async_remote_copy(
                src_ref=pos_in,
                dst_ref=halo_p.at[side],
                send_sem=hs_sem.at[2 + side],
                recv_sem=hr_sem.at[2 + side],
                device_id=to,
                device_id_type=MESH,
            ),
        )

    pl.semaphore_wait(barrier, has_nxt.astype(jnp.int32) + has_prv.astype(jnp.int32))

    for side, has, to in ((0, has_nxt, nxt_id), (1, has_prv, prv_id)):

        @pl.when(has)
        def _():
            for c in halo(side, to):
                c.start()

    for m in moves:
        m.wait()
    near_list[...] = inside(near_src[...] - (me - 1) * boxes, 3 * boxes)
    group_base = (lax.axis_index("box") - 1) * (2 * n_dir)
    src_list[...] = inside(trans_src[...] - group_base, 6 * n_dir)
    id_list[...] = inside(trans_id[...], ops)
    row = lax.broadcasted_iota(jnp.int32, (128, 512), 0)
    acc = jnp.zeros((128, 512), F)
    for s in range(4):
        acc = acc + jnp.where(idx[s : s + 1, :] == row, wgt[s : s + 1, :], 0.0)
    imat[...] = acc.astype(BF)

    leaf = jnp.dot(cur[...], rad[...], preferred_element_type=F).astype(BF)
    up_re = jnp.dot(leaf[:, :128], imat[...], preferred_element_type=F)
    up_im = jnp.dot(leaf[:, 128:], imat[...], preferred_element_type=F)
    turns = phase[...] * (1.0 / (2.0 * math.pi))
    cosv = cos_turns(turns)
    sinv = cos_turns(turns - 0.25)
    cosp[...] = cosv
    sinp[...] = sinv
    for q in range(2):
        re = jnp.zeros((8, 512), F)
        im = jnp.zeros((8, 512), F)
        for c in range(8):
            at = 64 * q + 8 * c
            cc, sc = cosv[c : c + 1, :], sinv[c : c + 1, :]
            ur, ui = up_re[at : at + 8], up_im[at : at + 8]
            re = re + (cc * ur - sc * ui)
            im = im + (sc * ur + cc * ui)
        both = jnp.concatenate([re, im], axis=0).astype(BF)
        for a in range(4):
            stage[a, q] = both[:, 128 * a : 128 * a + 128]

    width = 3 * boxes

    def tables(block, positions):
        def put(k, value):
            rows32[k * width + block * boxes : k * width + (block + 1) * boxes] = value

        def put_own(k, value):
            own32[k * boxes : (k + 1) * boxes] = value

        p = [positions[k].astype(F) for k in range(3)]
        norm = (p[0] * p[0] + p[1] * p[1] + p[2] * p[2]) * (TURN * TURN)
        parts = three_parts(norm)
        one = jnp.ones_like(norm)
        for k in range(3):
            for j in range(3):
                put(3 * j + k, p[k])
            put(9 + k, one)
            put(12 + k, parts[k])
        put(15, jnp.zeros_like(norm))
        if block == 1:
            for k in range(3):
                scaled = three_parts(p[k] * (-2.0 * TURN * TURN))
                for j in range(3):
                    put_own(3 * j + k, scaled[j])
                put_own(9 + k, parts[k])
                put_own(12 + k, one)
            put_own(15, jnp.zeros_like(norm))
        for i in range(boxes):
            src_tab[block * boxes + i] = rows32[pl.ds(block * boxes + i, 16, stride=width), :]

    def currents_of(block, values):
        for i in range(boxes // 2):
            pair = values[16 * i : 16 * i + 16].astype(F)
            for h in range(2):
                x_tab[block * boxes + 2 * i + h] = pair[8 * h : 8 * h + 8]

    tables(1, pos)
    currents_of(1, cur)
    for i in range(boxes):
        own_tab[i] = own32[pl.ds(i, 16, stride=boxes), :].T

    for i in range(boxes):
        tile = near_tile(distances(own_tab[i], [src_tab[boxes + i]]))
        near_self[i] = applied(tile, [x_tab[boxes + i]]).T[:8]

    for side, to_has, to, from_has in (
        (0, has_nxt, nxt_id, has_prv),
        (1, has_prv, prv_id, has_nxt),
    ):

        @pl.when(to_has)
        def _():
            for c in halo(side, to):
                c.wait_send()

        @pl.when(from_has)
        def _():
            for c in halo(side, to):
                c.wait_recv()

        @pl.when(jnp.logical_not(from_has))
        def _():
            halo_x[side] = jnp.zeros_like(halo_x[side])
            halo_p[side] = jnp.zeros_like(halo_p[side])

    for side in range(2):
        tables(2 * side, halo_p.at[side])
        currents_of(2 * side, halo_x.at[side])


def field_kernel(
    dims,
    near_list,
    src_list,
    id_list,
    src_tab,
    x_tab,
    own_tab,
    near_self,
    stage,
    imat,
    cosp,
    sinp,
    rad_in,
    count_in,
    table_in,
    out,
    rad,
    trans_src,
    trans_id,
    trans_count,
    tab,
    window,
    loc,
    back,
    near,
    ahead,
    in_sem,
    gs_sem,
    gr_sem,
    ss_sem,
    sr_sem,
    bs_sem,
    br_sem,
):
    n_box, n_dir, boxes, entries, trans_entries, ops = dims
    box = lax.axis_index("box")
    d = lax.axis_index("dir")
    quarter = lax.rem(d, 4)
    fourth = d // 4
    up_id = (lax.rem(box + 1, n_box), d)
    down_id = (lax.rem(box + n_box - 1, n_box), d)

    def peer(k):
        return lax.rem(d + k, n_dir)

    barrier = pltpu.get_barrier_semaphore()
    for to in (up_id, down_id):
        pl.semaphore_signal(barrier, inc=1, device_id=to, device_id_type=MESH)
    for k in range(1, n_dir):
        pl.semaphore_signal(barrier, inc=1, device_id=(box, peer(k)), device_id_type=MESH)

    lanes = pl.ds(pl.multiple_of(quarter * 128, 128), 128)
    moves = [
        pltpu.make_async_copy(a, b, in_sem.at[k])
        for k, (a, b) in enumerate(
            [
                (table_in.at[:, :, lanes], tab.at[pl.ds(0, ops)]),
                (src_list, trans_src),
                (id_list, trans_id),
                (count_in, trans_count),
                (rad_in, rad),
            ]
        )
    ]
    for m in moves:
        m.start()

    def group(k):
        to = peer(k)
        return pltpu.make_async_remote_copy(
            src_ref=stage.at[lax.rem(to, 4)],
            dst_ref=window.at[pl.ds(2 * n_dir + 2 * d, 2)],
            send_sem=gs_sem.at[k],
            recv_sem=gr_sem.at[k],
            device_id=(box, to),
            device_id_type=MESH,
        )

    def spread(side, to):
        return pltpu.make_async_remote_copy(
            src_ref=window.at[pl.ds(2 * n_dir, 2 * n_dir)],
            dst_ref=window.at[pl.ds(4 * n_dir * side, 2 * n_dir)],
            send_sem=ss_sem.at[side],
            recv_sem=sr_sem.at[side],
            device_id=to,
            device_id_type=MESH,
        )

    def returned(k):
        to = lax.rem(quarter + k, 4)
        return pltpu.make_async_remote_copy(
            src_ref=loc.at[to],
            dst_ref=back.at[quarter],
            send_sem=bs_sem.at[k],
            recv_sem=br_sem.at[k],
            device_id=(box, 4 * fourth + to),
            device_id_type=MESH,
        )

    def gather_start():
        pl.semaphore_wait(barrier, n_dir + 1)
        for k in range(1, n_dir):
            group(k).start()
        window[pl.ds(2 * n_dir + 2 * d, 2)] = stage[quarter]

    def spread_start():
        for k in range(1, n_dir):
            group(k).wait()
        spread(0, up_id).start()
        spread(1, down_id).start()

    def translate():
        spread(0, up_id).wait()
        spread(1, down_id).wait()
        for m in moves:
            m.wait()
        tab[ops] = jnp.zeros((2, 128), F)

        def target(r, inner):
            to = lax.rem(quarter + 1 + r // 2, 4)
            line = 8 * fourth + 2 * to + lax.rem(r, 2)
            count = trans_count[line]
            re = jnp.zeros((8, 128), F)
            im = jnp.zeros((8, 128), F)
            for e in range(trans_entries):
                op = jnp.where(e < count, trans_id[line, e], ops)
                src = window[trans_src[line, e]].astype(F)
                co = tab[op]
                cr, ci = co[0:1, :], co[1:2, :]
                re = re + (cr * src[:8] - ci * src[8:])
                im = im + (cr * src[8:] + ci * src[:8])
            loc[to, lax.rem(r, 2)] = jnp.concatenate([re, im], axis=0).astype(BF)
            return inner

        lax.fori_loop(0, 8, target, 0)
        for k in range(1, 4):
            returned(k).start()
        back[quarter] = loc[quarter]

    pairs = entries // 2

    def listed(ref, i, j):
        return [ref[near_list[i, e]] for e in range(2 * j + 1, min(2 * j + 3, entries))]

    def pair_distances(i, j):
        return distances(own_tab[i], listed(src_tab, i, j))

    steps = boxes // STRIDE
    first_half = jnp.logical_and(d >= 2, d < n_dir // 2)
    gather_at = jnp.where(d < 2, 1, jnp.where(d < 3 * n_dir // 8, 4, 2))
    spread_at = jnp.where(first_half, 6, 4)
    translate_at = jnp.where(first_half, steps, 6)

    def boxes_step(step, carry):
        pl.when(step == gather_at)(gather_start)
        pl.when(step == spread_at)(spread_start)
        pl.when(step == translate_at)(translate)
        tasks = [(STRIDE * step + h, j) for h in range(STRIDE) for j in range(pairs)]
        later = (jnp.minimum(STRIDE * (step + 1), boxes - 1), 0)
        dist = ahead[...]
        acc = None
        for t, (i, j) in enumerate(tasks):
            if t + 1 < len(tasks):
                dist_next = pair_distances(*tasks[t + 1])
            else:
                ahead[...] = pair_distances(*later)
            part = applied(near_tile(dist), listed(x_tab, i, j))
            acc = part if acc is None else acc + part
            if j == pairs - 1:
                near[i] = acc.T[:8]
                acc = None
            dist = dist_next
        return carry

    ahead[...] = pair_distances(0, 0)
    lax.fori_loop(0, steps, boxes_step, 0)
    pl.when(translate_at == steps)(translate)

    for k in range(1, 4):
        returned(k).wait()
    down_re, down_im = [], []
    for q in range(2):
        got = jnp.concatenate([back[a, q].astype(F) for a in range(4)], axis=1)
        lr, li = got[:8], got[8:]
        for c in range(8):
            cc, sc = cosp[c : c + 1, :], sinp[c : c + 1, :]
            down_re.append(cc * lr + sc * li)
            down_im.append(cc * li - sc * lr)
    in_re = lax.dot_general(
        jnp.concatenate(down_re, axis=0).astype(BF), imat[...], NT_DIMS, preferred_element_type=F
    )
    in_im = lax.dot_general(
        jnp.concatenate(down_im, axis=0).astype(BF), imat[...], NT_DIMS, preferred_element_type=F
    )
    incoming = jnp.concatenate([in_re, in_im], axis=1).astype(BF)
    far = lax.dot_general(incoming, rad[...], NT_DIMS, preferred_element_type=F)
    scale = 2.0 / math.sqrt(entries * 128)
    out[...] = (near[...] + near_self[...]).reshape(boxes * 8, 128) * scale + far


def in_hbm(x):
    return pltpu.with_memory_space_constraint(x, pltpu.HBM)


def per_device(
    currents,
    positions,
    radiation,
    interp_index,
    interp_weight,
    child_phase,
    near_src,
    trans_src,
    trans_id,
    trans_count,
    trans_table,
):
    boxes, waves, width = currents.shape
    n_box, n_dir = lax.axis_size("box"), lax.axis_size("dir")
    ops = trans_table.shape[0]
    smem = pl.BlockSpec(memory_space=pltpu.SMEM)
    vmem = pl.BlockSpec(memory_space=pltpu.VMEM)
    hbm = pl.BlockSpec(memory_space=pltpu.HBM)
    dma = pltpu.SemaphoreType.DMA
    shape = jax.ShapeDtypeStruct
    cur = currents.reshape(boxes * waves, width)
    pos = positions.transpose(1, 0, 2)
    idx = interp_index.T
    wgt = interp_weight.T
    prepared = pl.pallas_call(
        functools.partial(prepare_kernel, (n_box, n_dir, boxes, ops)),
        out_shape=[
            shape(near_src.shape, jnp.int32),
            shape(trans_src.shape, jnp.int32),
            shape(trans_id.shape, jnp.int32),
            shape((3 * boxes, 16, 128), F),
            shape((3 * boxes, 8, 128), F),
            shape((boxes, 128, 16), F),
            shape((boxes, 8, 128), F),
            shape((4, 2, 16, 128), BF),
            shape((128, 512), BF),
            shape((8, 512), F),
            shape((8, 512), F),
        ],
        in_specs=[hbm] * 9,
        out_specs=[vmem] * 11,
        scratch_shapes=[
            pltpu.VMEM(cur.shape, BF),
            pltpu.VMEM(pos.shape, BF),
            pltpu.VMEM(radiation.shape, BF),
            pltpu.VMEM(idx.shape, jnp.int32),
            pltpu.VMEM(wgt.shape, F),
            pltpu.VMEM(child_phase.shape, F),
            pltpu.VMEM(near_src.shape, jnp.int32),
            pltpu.VMEM(trans_src.shape, jnp.int32),
            pltpu.VMEM(trans_id.shape, jnp.int32),
            pltpu.VMEM((2,) + cur.shape, BF),
            pltpu.VMEM((2,) + pos.shape, BF),
            pltpu.VMEM((16 * 3 * boxes, 128), F),
            pltpu.VMEM((16 * boxes, 128), F),
            dma((9,)),
            dma((4,)),
            dma((4,)),
        ],
        compiler_params=pltpu.CompilerParams(
            collective_id=0, has_side_effects=True, vmem_limit_bytes=16 * 1024 * 1024
        ),
        name="prepare",
    )(
        *map(
            in_hbm,
            (cur, pos, radiation, idx, wgt, child_phase, near_src, trans_src, trans_id),
        )
    )
    dims = (n_box, n_dir, boxes, near_src.shape[1], trans_src.shape[1], ops)
    field = pl.pallas_call(
        functools.partial(field_kernel, dims),
        out_shape=shape((boxes * waves, width), F),
        in_specs=[smem] + [vmem] * 10 + [hbm] * 3,
        out_specs=vmem,
        scratch_shapes=[
            pltpu.VMEM(radiation.shape, BF),
            pltpu.SMEM(trans_src.shape, jnp.int32),
            pltpu.SMEM(trans_id.shape, jnp.int32),
            pltpu.SMEM(trans_count.shape, jnp.int32),
            pltpu.VMEM((ops + 1, 2, 128), F),
            pltpu.VMEM((6 * n_dir, 16, 128), BF),
            pltpu.VMEM((4, 2, 16, 128), BF),
            pltpu.VMEM((4, 2, 16, 128), BF),
            pltpu.VMEM((boxes, 8, 128), F),
            pltpu.VMEM((128, 256), F),
            dma((5,)),
            dma((16,)),
            dma((16,)),
            dma((2,)),
            dma((2,)),
            dma((4,)),
            dma((4,)),
        ],
        compiler_params=pltpu.CompilerParams(
            collective_id=1, has_side_effects=True, vmem_limit_bytes=32 * 1024 * 1024
        ),
        name="field",
    )(*prepared, *map(in_hbm, (radiation, trans_count, trans_table)))
    return field.reshape(boxes, waves, width)


def solution(mesh):
    placed = (
        P(("box", "dir"), None, None),
        P(("box", "dir"), None, None),
        P(),
        P(),
        P(),
        P(),
        P(("box", "dir"), None),
        P("box", None),
        P("box", None),
        P("box"),
        P(),
    )
    return jax.shard_map(
        per_device,
        mesh=mesh,
        in_specs=placed,
        out_specs=P(("box", "dir"), None, None),
        check_vma=False,
    )
```
